32 devices in a mesh: head: 2 (over x), blk: 16 (over z, y, core).
Axes of the slice: x: 2, y: 2, z: 4, core: 2. Of those that a mesh axis runs over, the one named last changes fastest.
Arguments:
- queries: bfloat16 [12288, 2560], P(('blk', 'head')), may hold values from -100 to 100
- key_rows: bfloat16 [12288, 2560], P(('blk', 'head')), may hold values from -4.5 to 4.5
- value_rows: bfloat16 [12288, 2560], P(('blk', 'head')), may hold values from -6 to 6
- key_tiles: int32 [96, 16], replicated, may hold values from 0 to 95, as said below
- tile_count: int32 [96], replicated, may hold values from 8 to 16, as said below
Outputs:
- attended: bfloat16 [12288, 2560], P(('blk', 'head'))
The draws below stay inside these ranges and needn't reach their ends.
Inputs may be any that keep to these rules, and one draw needn't show every extreme that they name: `key_tiles`: tile ids. Row q lists tile_count[q] distinct tiles first, the first being q itself; later entries equal q. With s = q // 6, every listed tile lies in slab s, in the upper half of slab s - 1, in the lower half of slab s + 1, or in slab s - 16 // 2**k or s + 16 // 2**k for k = 1 to 3; all query tiles of one slab that list a tile of such a distant slab list the same tile of it. `tile_count`: 16 is reached in every draw.
All inputs are finite; a program needn't handle non-finite values.
Results may differ from the reference program's by a relative error of at most 0.0034.
Values may be sent and summed in bfloat16 or wider, within the bound.
No kernel may reach another device: no remote copies, remote signals or barrier semaphores. Data moves between devices by JAX's collectives and lax.ppermute only.
A program may use at most 128 MiB of HBM per device.

```python
import math
import jax
import jax.numpy as jnp
from jax import lax

HD = 128
H = 20
TILE = 128
FAR = 3
TPS = 6
NSEL = 16
QTILES = 96
TOKENS = 12288
N_BLK = 16


def query_key_pair(key):
    base = jax.random.fold_in(key, 11)
    first_key, second_key = jax.random.split(base, 2)
    shape_full = (TOKENS, H * HD)
    key_values = jnp.clip(jax.random.normal(first_key, shape_full, jnp.float32), -4.5, 4.5)
    query_values = 2.2 * jnp.clip(jax.random.normal(second_key, shape_full, jnp.float32), -4.5, 4.5)
    return (query_values, key_values)


def draw_queries(key, part):
    return query_key_pair(key)[0].astype(jnp.bfloat16)


def draw_key_rows(key, part):
    return query_key_pair(key)[1].astype(jnp.bfloat16)


def mask_tables(key):
    base = jax.random.fold_in(key, 23)
    pick_key, order_key, count_key, slab_key, local_key = jax.random.split(base, 5)
    half_tiles = TPS // 2
    cand_total = 2 * TPS + 2 * FAR
    tile_ids = jnp.arange(QTILES, dtype=jnp.int32)
    slab_ids = tile_ids // TPS
    local_ids = tile_ids % TPS
    own_ids = slab_ids[:, None] * TPS + jnp.arange(TPS, dtype=jnp.int32)[None, :]
    own_valid = jnp.ones((QTILES, TPS), dtype=bool)
    prev_ids = (slab_ids[:, None] - 1) * TPS + half_tiles + jnp.arange(half_tiles, dtype=jnp.int32)[None, :]
    prev_valid = jnp.broadcast_to((slab_ids > 0)[:, None], (QTILES, half_tiles))
    next_ids = (slab_ids[:, None] + 1) * TPS + jnp.arange(half_tiles, dtype=jnp.int32)[None, :]
    next_valid = jnp.broadcast_to((slab_ids < N_BLK - 1)[:, None], (QTILES, half_tiles))
    picks = jax.random.randint(pick_key, (N_BLK, 2 * FAR), 0, TPS, dtype=jnp.int32)
    far_ids = []
    far_valid = []
    for level_index in range(1, FAR + 1):
        distance = N_BLK // 2 ** level_index
        for side_index, direction in enumerate((-1, 1)):
            target = slab_ids + direction * distance
            column = picks[slab_ids, 2 * (level_index - 1) + side_index]
            far_ids.append((target * TPS + column)[:, None])
            far_valid.append(((target >= 0) & (target < N_BLK))[:, None])
    cand_ids = jnp.concatenate([own_ids, prev_ids, next_ids] + far_ids, axis=1)
    cand_valid = jnp.concatenate([own_valid, prev_valid, next_valid] + far_valid, axis=1)
    noise = jax.random.randint(order_key, (QTILES, cand_total), 0, 1 << 20, dtype=jnp.int32)
    cand_cols = jnp.arange(cand_total, dtype=jnp.int32)
    rank_score = noise * cand_total + cand_cols[None, :]
    rank_score = jnp.where(cand_cols[None, :] == local_ids[:, None], 1 << 30, rank_score)
    rank_score = jnp.where(cand_valid, rank_score, -1)
    order = jnp.argsort(-rank_score, axis=1, stable=True)[:, :NSEL]
    chosen = jnp.take_along_axis(cand_ids, order, axis=1)
    available = jnp.sum(cand_valid.astype(jnp.int32), axis=1)
    counts = jax.random.randint(count_key, (QTILES,), NSEL // 2, NSEL + 1, dtype=jnp.int32)
    counts = jnp.minimum(counts, available)
    forced_slab = jax.random.randint(slab_key, (), N_BLK // 4, 3 * N_BLK // 4, dtype=jnp.int32)
    forced_local = jax.random.randint(local_key, (), 0, TPS, dtype=jnp.int32)
    counts = jnp.where(tile_ids == forced_slab * TPS + forced_local, NSEL, counts)
    live_slots = jnp.arange(NSEL, dtype=jnp.int32)[None, :] < counts[:, None]
    listed = jnp.where(live_slots, chosen, tile_ids[:, None])
    return (listed.astype(jnp.int32), counts.astype(jnp.int32))


def draw_key_tiles(key, part):
    return mask_tables(key)[0]


def draw_tile_count(key, part):
    return mask_tables(key)[1]


def block_levels(own_key, shape, cuts, smallest, top_value):
    def one(dim, blocks):
        draws = jax.random.uniform(jax.random.fold_in(jax.random.fold_in(own_key, 6), dim), (blocks,), jnp.float32, smallest / len(cuts), top_value / len(cuts))
        return jnp.repeat(jnp.exp(draws), shape[dim] // blocks).reshape((-1,) + (1,) * (len(shape) - dim - 1))

    factor_of = one(*cuts[0])
    for cut in cuts[1:]:
        factor_of = factor_of * one(*cut)
    return factor_of


def bell_draw(key, extent, deviation, most, cuts=(), held_as=jnp.bfloat16):
    loudness = block_levels(key, extent, cuts, -0.22, 0.18) if cuts else 1.0
    values = jax.random.normal(key, extent, jnp.float32) * deviation * loudness
    return jnp.minimum(jnp.maximum(values, -most), most).astype(held_as)


def setup_inputs(seed: int = 0) -> dict:
    arg_keys = jax.random.split(jax.random.key(seed), 6)
    queries = draw_queries(jax.random.fold_in(arg_keys[5], 71), 0)
    key_rows = draw_key_rows(jax.random.fold_in(arg_keys[5], 71), 0)
    value_rows = bell_draw(arg_keys[2], (TOKENS, H * HD), 1.0, 6.0, ((0, 32),))
    key_tiles = draw_key_tiles(jax.random.fold_in(arg_keys[5], 71), 0)
    tile_count = draw_tile_count(jax.random.fold_in(arg_keys[5], 71), 0)
    return dict(queries=queries, key_rows=key_rows, value_rows=value_rows, key_tiles=key_tiles, tile_count=tile_count)


masked_value = -1e+30

def reference(queries, key_rows, value_rows, key_tiles, tile_count):
    row_width = H * HD
    score_scale = 1.0 / math.sqrt(HD)
    query_tiles = queries.reshape(QTILES, TILE, row_width)
    key_stack = key_rows.reshape(QTILES, TILE, row_width)
    value_stack = value_rows.reshape(QTILES, TILE, row_width)

    def attend_tile(tile_index):
        query_part = query_tiles[tile_index].astype(jnp.float32).reshape(TILE, H, HD)
        listed = key_tiles[tile_index]
        key_part = key_stack[listed].astype(jnp.float32).reshape(NSEL * TILE, H, HD)
        value_part = value_stack[listed].astype(jnp.float32).reshape(NSEL * TILE, H, HD)
        live_slots = jnp.arange(NSEL, dtype=jnp.int32) < tile_count[tile_index]
        live_rows = jnp.repeat(live_slots, TILE)
        scores = jnp.einsum('qhd,khd->hqk', query_part, key_part) * score_scale
        scores = jnp.where(live_rows[None, None, :], scores, masked_value)
        largest = lax.optimization_barrier(jnp.max(scores, axis=-1, keepdims=True))
        weights = jnp.exp(scores - largest)
        totals = lax.optimization_barrier(jnp.sum(weights, axis=-1))
        rounded = weights.astype(jnp.bfloat16)
        rounded = lax.optimization_barrier(rounded).astype(jnp.float32)
        mixture = jnp.einsum('hqk,khd->qhd', rounded, value_part)
        mixture = mixture / jnp.transpose(totals)[:, :, None]
        return mixture.reshape(TILE, row_width).astype(jnp.bfloat16)
    result = lax.map(attend_tile, jnp.arange(QTILES, dtype=jnp.int32))
    return result.reshape(TOKENS, row_width)
```

```python
import functools
import math

import jax
import jax.numpy as jnp
from jax import lax
from jax.experimental import pallas as pl
from jax.experimental.pallas import tpu as pltpu
from jax.sharding import PartitionSpec as P

HD = 128
TILE = 128
FAR = 3


masked_value = -1e30
exp2_scale = math.log2(math.e) / math.sqrt(HD)
across = (((1,), (1,)), ((), ()))
anywhere = pl.BlockSpec(memory_space=pl.ANY)


def copy_block(where, *refs):
    count = len(refs) - 1
    out = refs[-1]
    for i in range(count):
        out[i] = refs[i][...]


def pack_columns(arrays, first_block, width, rows):
    total = arrays[0].shape[0]
    return pl.pallas_call(
        copy_block,
        out_shape=jax.ShapeDtypeStruct((len(arrays), total, width), arrays[0].dtype),
        grid_spec=pltpu.PrefetchScalarGridSpec(
            num_scalar_prefetch=1,
            grid=(total // rows,),
            in_specs=[pl.BlockSpec((rows, width), lambda i, w: (i, w[0]))] * len(arrays),
            out_specs=pl.BlockSpec((len(arrays), rows, width), lambda i, w: (0, i, 0)),
        ),
    )(first_block, *arrays)


def distant_kernel(half, low_col, width, meta, key, value, received, *rest):
    count = (len(rest) - 1) // 1
    outs, sems = rest[:-1], rest[-1]
    group_width = meta[0]
    first = pl.multiple_of(meta[0] * width_of(key) + low_col, HD)
    copies = []
    for i, out in enumerate(outs):
        slot = meta[1 + i]
        own = slot < half
        rows = pl.ds(pl.multiple_of(lax.rem(slot, half) * TILE, TILE), TILE)
        cols = pl.ds(first, width)
        for j, source in enumerate((key, value)):
            sem = sems.at[i, j]
            mine = pltpu.make_async_copy(source.at[rows, cols], out.at[j], sem)
            theirs = pltpu.make_async_copy(received.at[j, rows, :], out.at[j], sem)
            pl.when(own)(mine.start)
            pl.when(jnp.logical_not(own))(theirs.start)
            copies.append(theirs)
    for copy in copies:
        copy.wait()


def width_of(ref):
    return ref.shape[1] // 2


def select_distant(meta, key, value, received, low_col, count, half):
    width = received.shape[2]
    shape = jax.ShapeDtypeStruct((2, TILE, width), key.dtype)
    return pl.pallas_call(
        functools.partial(distant_kernel, half, low_col, width),
        out_shape=[shape] * count,
        grid_spec=pltpu.PrefetchScalarGridSpec(
            num_scalar_prefetch=1,
            grid=(),
            in_specs=[anywhere] * 3,
            out_specs=[anywhere] * count,
            scratch_shapes=[pltpu.SemaphoreType.DMA((count, 2))],
        ),
    )(meta, key, value, received)


def attend_kernel(allowed, where, q_own, q_rec, k_own, v_own, kv_rec, rim_a, rim_b, *rest):
    far, (o_own, o_send) = rest[:-2], rest[-2:]
    tiles = q_own.shape[0] // TILE
    keys = jnp.concatenate([k_own[...], kv_rec[0], rim_a[0], rim_b[0]] + [d[0] for d in far], 0)
    values = jnp.concatenate([v_own[...], kv_rec[1], rim_a[1], rim_b[1]] + [d[1] for d in far], 0)
    slots = keys.shape[0] // TILE
    for q_ref, o_ref, base in ((q_own, o_own, 0), (q_rec, o_send, tiles)):
        scores = lax.dot_general(q_ref[...], keys, across, preferred_element_type=jnp.float32)
        rounded, totals = [], []
        for t in range(tiles):
            rows = slice(t * TILE, (t + 1) * TILE)
            cells = [
                jnp.where(
                    allowed[base + t, j] > 0,
                    scores[rows, j * TILE : (j + 1) * TILE],
                    masked_value,
                )
                for j in range(slots)
            ]
            largest = jnp.max(functools.reduce(jnp.maximum, cells), -1, keepdims=True)
            weights = [jnp.exp2((cell - largest) * exp2_scale) for cell in cells]
            totals.append(jnp.sum(functools.reduce(jnp.add, weights), -1, keepdims=True))
            rounded.append(jnp.concatenate([w.astype(jnp.bfloat16) for w in weights], 1))
        mixture = jnp.dot(
            jnp.concatenate(rounded, 0), values, preferred_element_type=jnp.float32
        )
        o_ref[...] = (mixture / jnp.concatenate(totals, 0)).astype(o_ref.dtype)


def attend(allowed, where, arrays, chunk_low, low, high, heads_here):
    queries, q_rec, key, value, kv_rec, rim_a, rim_b, far = arrays
    rows = queries.shape[0]
    own = pl.BlockSpec((rows, HD), lambda i, a, w: (0, w[0] * heads_here + low + i))
    flat = pl.BlockSpec((rows, HD), lambda i, a, w: (0, low + i))
    whole = pl.BlockSpec((2, rows, HD), lambda i, a, w: (0, 0, low + i))
    part = pl.BlockSpec((2, rows, HD), lambda i, a, w: (0, 0, low - chunk_low + i))
    tile = pl.BlockSpec((2, TILE, HD), lambda i, a, w: (0, 0, low - chunk_low + i))
    out = pl.BlockSpec((rows, HD), lambda i, a, w: (0, i))
    shape = jax.ShapeDtypeStruct((rows, (high - low) * HD), queries.dtype)
    return pl.pallas_call(
        attend_kernel,
        out_shape=[shape, shape],
        grid_spec=pltpu.PrefetchScalarGridSpec(
            num_scalar_prefetch=2,
            grid=(high - low,),
            in_specs=[own, flat, own, own, part, whole, part] + [tile] * len(far),
            out_specs=[out, out],
        ),
    )(allowed, where, queries, q_rec, key, value, kv_rec, rim_a, rim_b, *far)


def place_kernel(pieces, where, *refs):
    ins, out, sems = refs[:-2], refs[-2], refs[-1]
    group = out.shape[1] // 2
    copies = []
    for i, (low, mine) in enumerate(pieces):
        side = where[0] if mine else 1 - where[0]
        cols = pl.ds(pl.multiple_of(side * group + low, HD), ins[i].shape[1])
        copies.append(pltpu.make_async_copy(ins[i], out.at[:, cols], sems.at[i]))
    for copy in copies:
        copy.start()
    for copy in copies:
        copy.wait()


def place(where, pieces, arrays, shape):
    return pl.pallas_call(
        functools.partial(place_kernel, pieces),
        out_shape=shape,
        grid_spec=pltpu.PrefetchScalarGridSpec(
            num_scalar_prefetch=1,
            grid=(),
            in_specs=[anywhere] * len(arrays),
            out_specs=anywhere,
            scratch_shapes=[pltpu.SemaphoreType.DMA((len(arrays),))],
        ),
    )(where, *arrays)


def on_device(queries, key_rows, value_rows, key_tiles, tile_count):
    tok_rows, row_width = queries.shape
    side = lax.axis_index("head")
    slab = lax.axis_index("blk")
    slabs = lax.axis_size("blk")
    group_width = row_width // 2
    heads_here = group_width // HD
    half = tok_rows // TILE
    slab_tiles = 2 * half

    shifts = [(0, slabs // 2)]
    for level in range(2, FAR + 1):
        shifts += [(1, slabs // 2**level), (-1, slabs // 2**level)]
    live = jnp.arange(key_tiles.shape[1], dtype=jnp.int32)[None, :] < tile_count[:, None]
    listed_slab = key_tiles // slab_tiles
    within = key_tiles % slab_tiles
    turned = (within + half * side) % slab_tiles
    mine = jnp.where(live & (listed_slab == slab), turned, 0)
    chosen = jnp.max(mine.reshape(slabs, -1), axis=1)
    readers = [
        (slab + shifts[0][1]) % slabs if direction == 0 else jnp.clip(slab + direction * far, 0, slabs - 1)
        for direction, far in shifts
    ]
    sent_slots = chosen[jnp.stack(readers)]
    where = side.astype(jnp.int32)[None]
    meta = jnp.concatenate([where, sent_slots])

    offset = listed_slab - slab
    slots = jnp.where(offset == 0, turned, -1)
    slots = jnp.where(offset == -1, 2 * half + half * (1 - side) + within - half, slots)
    slots = jnp.where(offset == 1, 2 * half + half * side + within, slots)
    for i, (direction, far) in enumerate(shifts):
        hit = (jnp.abs(offset) == far) if direction == 0 else (offset == -direction * far)
        slots = jnp.where(hit, 4 * half + i, slots)
    slots = jnp.where(live, slots, -1)
    slots = lax.dynamic_slice_in_dim(slots, slab * slab_tiles, slab_tiles, 0)
    slots = jnp.where(side == 0, slots, jnp.roll(slots, half, axis=0))
    slot_total = 4 * half + len(shifts)
    allowed = jnp.any(
        slots[:, :, None] == jnp.arange(slot_total, dtype=jnp.int32)[None, None, :], axis=1
    ).astype(jnp.int32)

    swap = [(0, 1), (1, 0)]
    chunks = [(0, heads_here // 2), (heads_here // 2, heads_here)]
    other = 1 - where

    def outward(direction):
        return [
            (g * slabs + s, g * slabs + s + step)
            for g, step in ((0, -direction), (1, direction))
            for s in range(slabs)
            if 0 <= s + step < slabs
        ]

    kv_rec = []
    for low, high in chunks:
        width = (high - low) * HD
        packed = pack_columns(
            [key_rows, value_rows], other * (group_width // width) + low * HD // width, width, TILE
        )
        kv_rec.append(lax.ppermute(packed, "head", swap))
    rim_a = lax.ppermute(
        pack_columns([key_rows, value_rows], where, group_width, TILE),
        ("head", "blk"),
        outward(1),
    )
    q_rec = lax.ppermute(
        pack_columns([queries], other, group_width, TILE), "head", swap
    )[0]

    own_pieces, sent_pieces, spots = [], [], []
    for c, (low, high) in enumerate(chunks):
        rim_b = lax.ppermute(kv_rec[c], ("head", "blk"), outward(-1))
        tiles = select_distant(
            meta, key_rows, value_rows, kv_rec[c], low * HD, len(shifts), half
        )
        far = []
        for (direction, distance), tile in zip(shifts, tiles):
            if direction == 0:
                pairs = [(s, (s + distance) % slabs) for s in range(slabs)]
            else:
                step = direction * distance
                pairs = [(s, s + step) for s in range(slabs) if 0 <= s + step < slabs]
            far.append(lax.ppermute(tile, "blk", pairs))
        arrays = (queries, q_rec, key_rows, value_rows, kv_rec[c], rim_a, rim_b, far)
        cuts = list(range(low, high, 2)) + [high]
        for a, b in zip(cuts[:-1], cuts[1:]):
            o_own, o_send = attend(allowed, where, arrays, low, a, b, heads_here)
            own_pieces.append(o_own)
            sent_pieces.append(lax.ppermute(o_send, "head", swap))
            spots.append(a * HD)
    return place(
        where,
        [(s, True) for s in spots] + [(s, False) for s in spots],
        own_pieces + sent_pieces,
        jax.ShapeDtypeStruct(queries.shape, queries.dtype),
    )


def solution(mesh):
    placed = (
        P(("blk", "head"), None),
        P(("blk", "head"), None),
        P(("blk", "head"), None),
        P(),
        P(),
    )
    return jax.shard_map(
        on_device, mesh=mesh, in_specs=placed, out_specs=P(("blk", "head"), None), check_vma=False
    )
```

```python
import functools
import math

import jax
import jax.numpy as jnp
from jax import lax
from jax.experimental import pallas as pl
from jax.experimental.pallas import tpu as pltpu
from jax.sharding import PartitionSpec as P


HD = 128
TILE = 128
FAR = 3


masked_value = -1e30
exp2_scale = math.log2(math.e) / math.sqrt(HD)
across = (((1,), (1,)), ((), ()))
anywhere = pl.BlockSpec(memory_space=pl.ANY)


def columns_of(array, side, low, width):
    half = array.shape[1] // 2
    first = lax.slice_in_dim(array, low, low + width, axis=1)
    second = lax.slice_in_dim(array, half + low, half + low + width, axis=1)
    return jnp.where(side == 0, first, second)


def distant_kernel(half, low_col, width, meta, key, value, received, *rest):
    outs, sems = rest[:-1], rest[-1]
    first = pl.multiple_of(meta[0] * width_of(key) + low_col, HD)
    copies = []
    for i, out in enumerate(outs):
        slot = meta[1 + i]
        own = slot < half
        rows = pl.ds(pl.multiple_of(lax.rem(slot, half) * TILE, TILE), TILE)
        cols = pl.ds(first, width)
        for j, source in enumerate((key, value)):
            sem = sems.at[i, j]
            mine = pltpu.make_async_copy(source.at[rows, cols], out.at[j], sem)
            theirs = pltpu.make_async_copy(received.at[j, rows, :], out.at[j], sem)
            pl.when(own)(mine.start)
            pl.when(jnp.logical_not(own))(theirs.start)
            copies.append(theirs)
    for copy in copies:
        copy.wait()


def width_of(ref):
    return ref.shape[1] // 2


def select_distant(meta, key, value, received, low_col, count, half):
    width = received.shape[2]
    shape = jax.ShapeDtypeStruct((2, TILE, width), key.dtype)
    return pl.pallas_call(
        functools.partial(distant_kernel, half, low_col, width),
        out_shape=[shape] * count,
        grid_spec=pltpu.PrefetchScalarGridSpec(
            num_scalar_prefetch=1,
            grid=(),
            in_specs=[anywhere] * 3,
            out_specs=[pl.BlockSpec(memory_space=pltpu.VMEM)] * count,
            scratch_shapes=[pltpu.SemaphoreType.DMA((count, 2))],
        ),
    )(meta, key, value, received)


def attend_kernel(allowed, where, q_own, q_rec, k_own, v_own, kv_rec, rim_a, rim_b, *rest):
    far, (o_own, o_send) = rest[:-2], rest[-2:]
    tiles = q_own.shape[0] // TILE
    keys = jnp.concatenate([k_own[...], kv_rec[0], rim_a[0], rim_b[0]] + [d[0] for d in far], 0)
    values = jnp.concatenate([v_own[...], kv_rec[1], rim_a[1], rim_b[1]] + [d[1] for d in far], 0)
    slots = keys.shape[0] // TILE
    for q_ref, o_ref, base in ((q_own, o_own, 0), (q_rec, o_send, tiles)):
        scores = lax.dot_general(q_ref[...], keys, across, preferred_element_type=jnp.float32)
        rounded, totals = [], []
        for t in range(tiles):
            rows = slice(t * TILE, (t + 1) * TILE)
            cells = [
                jnp.where(
                    allowed[base + t, j] > 0,
                    scores[rows, j * TILE : (j + 1) * TILE],
                    masked_value,
                )
                for j in range(slots)
            ]
            largest = jnp.max(functools.reduce(jnp.maximum, cells), -1, keepdims=True)
            weights = [jnp.exp2((cell - largest) * exp2_scale) for cell in cells]
            totals.append(jnp.sum(functools.reduce(jnp.add, weights), -1, keepdims=True))
            rounded.append(jnp.concatenate([w.astype(jnp.bfloat16) for w in weights], 1))
        mixture = jnp.dot(
            jnp.concatenate(rounded, 0), values, preferred_element_type=jnp.float32
        )
        o_ref[...] = (mixture / jnp.concatenate(totals, 0)).astype(o_ref.dtype)


def attend(allowed, where, arrays, result, chunk_low, low, high, heads_here):
    queries, q_rec, key, value, kv_rec, rim_a, rim_b, far = arrays
    rows = queries.shape[0]
    own = pl.BlockSpec((rows, HD), lambda i, a, w: (0, w[0] * heads_here + low + i))
    flat = pl.BlockSpec((rows, HD), lambda i, a, w: (0, low + i))
    whole = pl.BlockSpec((2, rows, HD), lambda i, a, w: (0, 0, low + i))
    part = pl.BlockSpec((2, rows, HD), lambda i, a, w: (0, 0, low - chunk_low + i))
    tile = pl.BlockSpec((2, TILE, HD), lambda i, a, w: (0, 0, low - chunk_low + i))
    out = pl.BlockSpec((rows, HD), lambda i, a, w: (0, i))
    shape = jax.ShapeDtypeStruct((rows, (high - low) * HD), queries.dtype)
    inputs = [queries, q_rec, key, value, kv_rec, rim_a, rim_b, *far]
    specs = [own, flat, own, own, part, whole, part] + [tile] * len(far)
    aliases = {}
    kernel = attend_kernel
    if result is not None:
        kernel = functools.partial(skip_operand, attend_kernel, 2 + len(inputs))
        aliases = {2 + len(inputs): 0}
        inputs, specs = inputs + [result], specs + [anywhere]
    return pl.pallas_call(
        kernel,
        out_shape=[jax.ShapeDtypeStruct(queries.shape, queries.dtype), shape],
        grid_spec=pltpu.PrefetchScalarGridSpec(
            num_scalar_prefetch=2,
            grid=(high - low,),
            in_specs=specs,
            out_specs=[own, out],
        ),
        input_output_aliases=aliases,
    )(allowed, where, *inputs)


def skip_operand(kernel, index, *refs):
    kernel(*refs[:index], *refs[index + 1 :])


def place_kernel(lows, heads_here, where, *refs):
    count = len(lows)
    pieces, out, held, sems = refs[:count], refs[count + 1], refs[count + 2 : -1], refs[-1]
    loads, stores = [], []
    for i, low in enumerate(lows):
        cols = pl.ds(pl.multiple_of(((1 - where[0]) * heads_here + low) * HD, HD), held[i].shape[1])
        loads.append(pltpu.make_async_copy(pieces[i], held[i], sems.at[0, i]))
        stores.append(pltpu.make_async_copy(held[i], out.at[:, cols], sems.at[1, i]))
    for load in loads:
        load.start()
    for load, store in zip(loads, stores):
        load.wait()
        store.start()
    for store in stores:
        store.wait()


def place(where, pieces, lows, result, heads_here):
    return pl.pallas_call(
        functools.partial(place_kernel, lows, heads_here),
        out_shape=jax.ShapeDtypeStruct(result.shape, result.dtype),
        grid_spec=pltpu.PrefetchScalarGridSpec(
            num_scalar_prefetch=1,
            grid=(),
            in_specs=[anywhere] * (len(pieces) + 1),
            out_specs=anywhere,
            scratch_shapes=[pltpu.VMEM(piece.shape, piece.dtype) for piece in pieces]
            + [pltpu.SemaphoreType.DMA((2, len(pieces)))],
        ),
        input_output_aliases={1 + len(pieces): 0},
    )(where, *pieces, result)


def on_device(queries, key_rows, value_rows, key_tiles, tile_count):
    tok_rows, row_width = queries.shape
    side = lax.axis_index("head")
    slab = lax.axis_index("blk")
    slabs = lax.axis_size("blk")
    group_width = row_width // 2
    heads_here = group_width // HD
    half = tok_rows // TILE
    slab_tiles = 2 * half

    shifts = [(0, slabs // 2)]
    for level in range(2, FAR + 1):
        shifts += [(1, slabs // 2**level), (-1, slabs // 2**level)]
    live = jnp.arange(key_tiles.shape[1], dtype=jnp.int32)[None, :] < tile_count[:, None]
    listed_slab = key_tiles // slab_tiles
    within = key_tiles % slab_tiles
    turned = (within + half * side) % slab_tiles
    mine = jnp.where(live & (listed_slab == slab), turned, 0)
    chosen = jnp.max(mine.reshape(slabs, -1), axis=1)
    readers = [
        (slab + shifts[0][1]) % slabs if direction == 0 else jnp.clip(slab + direction * far, 0, slabs - 1)
        for direction, far in shifts
    ]
    sent_slots = chosen[jnp.stack(readers)]
    where = side.astype(jnp.int32)[None]
    meta = jnp.concatenate([where, sent_slots])

    offset = listed_slab - slab
    slots = jnp.where(offset == 0, turned, -1)
    slots = jnp.where(offset == -1, 2 * half + half * (1 - side) + within - half, slots)
    slots = jnp.where(offset == 1, 2 * half + half * side + within, slots)
    for i, (direction, far) in enumerate(shifts):
        hit = (jnp.abs(offset) == far) if direction == 0 else (offset == -direction * far)
        slots = jnp.where(hit, 4 * half + i, slots)
    slots = jnp.where(live, slots, -1)
    slots = lax.dynamic_slice_in_dim(slots, slab * slab_tiles, slab_tiles, 0)
    slots = jnp.where(side == 0, slots, jnp.roll(slots, half, axis=0))
    slot_total = 4 * half + len(shifts)
    allowed = jnp.any(
        slots[:, :, None] == jnp.arange(slot_total, dtype=jnp.int32)[None, None, :], axis=1
    ).astype(jnp.int32)

    swap = [(0, 1), (1, 0)]
    chunks = chunk_bounds(heads_here)

    def outward(direction):
        return [
            (g * slabs + s, g * slabs + s + step)
            for g, step in ((0, -direction), (1, direction))
            for s in range(slabs)
            if 0 <= s + step < slabs
        ]

    kv_rec = []
    rim_a = None
    for c, (low, high) in enumerate(chunks):
        width = (high - low) * HD
        packed = jnp.stack(
            [columns_of(array, 1 - side, low * HD, width) for array in (key_rows, value_rows)]
        )
        kv_rec.append(lax.ppermute(packed, "head", swap))
        if c == 0:
            rim_a = lax.ppermute(
                jnp.stack(
                    [columns_of(array, side, 0, group_width) for array in (key_rows, value_rows)]
                ),
                ("head", "blk"),
                outward(1),
            )
    q_rec = lax.ppermute(columns_of(queries, 1 - side, 0, group_width), "head", swap)

    gathered = []
    for c, (low, high) in enumerate(chunks):
        rim_b = lax.ppermute(kv_rec[c], ("head", "blk"), outward(-1))
        tiles = select_distant(meta, key_rows, value_rows, kv_rec[c], low * HD, len(shifts), half)
        far = []
        for (direction, distance), tile in zip(shifts, tiles):
            if direction == 0:
                pairs = [(s, (s + distance) % slabs) for s in range(slabs)]
            else:
                step = direction * distance
                pairs = [(s, s + step) for s in range(slabs) if 0 <= s + step < slabs]
            far.append(lax.ppermute(tile, "blk", pairs))
        gathered.append((rim_b, far))
    result, returned = None, []
    for c, a, b in head_runs(heads_here):
        rim_b, far = gathered[c]
        arrays = (queries, q_rec, key_rows, value_rows, kv_rec[c], rim_a, rim_b, far)
        result, sent = attend(allowed, where, arrays, result, chunks[c][0], a, b, heads_here)
        returned.append((a, lax.ppermute(sent, "head", swap)))
    result = place(
        where, [p for _, p in returned[:-1]], [a for a, _ in returned[:-1]], result, heads_here
    )
    result = place(where, [returned[-1][1]], [returned[-1][0]], result, heads_here)
    return result


def chunk_bounds(heads):
    cuts = [0, heads * 3 // 10, heads * 7 // 10, heads]
    return list(zip(cuts[:-1], cuts[1:]))


def head_runs(heads):
    runs = []
    for c, (low, high) in enumerate(chunk_bounds(heads)):
        cuts = [low, high] if c == 0 else [low, low + (high - low + 1) // 2, high]
        runs += [(c, a, b) for a, b in zip(cuts[:-1], cuts[1:])]
    return runs


def solution(mesh):
    placed = (
        P(("blk", "head"), None),
        P(("blk", "head"), None),
        P(("blk", "head"), None),
        P(),
        P(),
    )

    return jax.shard_map(
        on_device, mesh=mesh, in_specs=placed, out_specs=P(("blk", "head"), None), check_vma=False
    )
```

```python
import functools
import math

import jax
import jax.numpy as jnp
from jax import lax
from jax.experimental import pallas as pl
from jax.experimental.pallas import tpu as pltpu
from jax.sharding import PartitionSpec as P


HD = 128
TILE = 128
FAR = 3


masked_value = -1e30
exp2_scale = math.log2(math.e) / math.sqrt(HD)
across = (((1,), (1,)), ((), ()))
anywhere = pl.BlockSpec(memory_space=pl.ANY)


def columns_of(array, side, low, width):
    half = array.shape[1] // 2
    first = lax.slice_in_dim(array, low, low + width, axis=1)
    second = lax.slice_in_dim(array, half + low, half + low + width, axis=1)
    return jnp.where(side == 0, first, second)


def distant_kernel(half, low_col, meta, key, value, *rest):
    count = meta.shape[0] - 1
    received, outs, sems = rest[: -count - 1], rest[-count - 1 : -1], rest[-1]
    side_col = meta[0] * (key.shape[1] // 2) + low_col
    waits = []
    for i, out in enumerate(outs):
        slot = meta[1 + i]
        own = slot < half
        rows = pl.ds(pl.multiple_of(lax.rem(slot, half) * TILE, TILE), TILE)
        first = 0
        for p, part in enumerate(received):
            width = part.shape[2]
            cols = pl.ds(pl.multiple_of(side_col + first, HD), width)
            for j, source in enumerate((key, value)):
                target, sem = out.at[j, :, first : first + width], sems.at[i, j, p]
                mine = pltpu.make_async_copy(source.at[rows, cols], target, sem)
                theirs = pltpu.make_async_copy(part.at[j, rows, :], target, sem)
                pl.when(own)(mine.start)
                pl.when(jnp.logical_not(own))(theirs.start)
                waits.append(theirs)
            first += width
    for copy in waits:
        copy.wait()


def select_distant(meta, key, value, received, low_col, half):
    count = meta.shape[0] - 1
    width = sum(part.shape[2] for part in received)
    shape = pltpu.VMEM((2, TILE, width), key.dtype)
    return pl.pallas_call(
        functools.partial(distant_kernel, half, low_col),
        out_shape=[shape] * count,
        grid_spec=pltpu.PrefetchScalarGridSpec(
            num_scalar_prefetch=1,
            grid=(),
            in_specs=[anywhere] * (2 + len(received)),
            out_specs=[pl.BlockSpec(memory_space=pltpu.VMEM)] * count,
            scratch_shapes=[pltpu.SemaphoreType.DMA((count, 2, len(received)))],
        ),
    )(meta, key, value, *received)


def attend_kernel(allowed, where, q_own, q_rec, k_own, v_own, kv_rec, rim_a, rim_b, *rest):
    far, (o_own, o_send, keys, values, scores, tops) = rest[:-6], rest[-6:]
    rows = q_own.shape[0]
    tiles = rows // TILE
    slots = keys.shape[0] // TILE

    @pl.when(pl.program_id(0) == 0)
    def fill_ones():
        values[:, HD:] = jnp.ones((slots * TILE, HD), values.dtype)

    first = 0
    sources = [(k_own[...], v_own[...])]
    sources += [(ref[0], ref[1]) for ref in (kv_rec, rim_a, rim_b, *far)]
    for key_part, value_part in sources:
        last = first + key_part.shape[0]
        keys[first:last, :] = key_part
        values[first:last, :HD] = value_part
        first = last

    pairs = [(j, min(j + 2, slots)) for j in range(0, slots, 2)]
    blocks = [(q_own, o_own, t, t) for t in range(tiles)]
    blocks += [(q_rec, o_send, t, tiles + t) for t in range(tiles)]
    largest, mixed = {}, {}

    def score(b, pair):
        q_ref, _, t, row = blocks[b]
        low, high = pair
        cells = lax.dot_general(
            q_ref[t * TILE : (t + 1) * TILE, :],
            keys[low * TILE : high * TILE, :],
            across,
            preferred_element_type=jnp.float32,
        )
        for j in range(low, high):
            cell = cells[:, (j - low) * TILE : (j - low + 1) * TILE]
            cell = jnp.where(allowed[row, j] > 0, cell, masked_value)
            scores[b % 2, :, j * TILE : (j + 1) * TILE] = cell
            largest[b] = cell if b not in largest else jnp.maximum(largest[b], cell)

    def settle(b):
        top = jnp.max(largest[b], axis=-1, keepdims=True)
        tops[b % 2] = jnp.broadcast_to(top, (TILE, TILE))

    def mix(b, pair):
        low, high = pair
        rounded = [
            jnp.exp2(
                (scores[b % 2, :, j * TILE : (j + 1) * TILE] - tops[b % 2]) * exp2_scale
            ).astype(values.dtype)
            for j in range(low, high)
        ]
        part = jnp.dot(
            jnp.concatenate(rounded, 1),
            values[low * TILE : high * TILE, :],
            preferred_element_type=jnp.float32,
        )
        mixed[b] = part if b not in mixed else mixed[b] + part

    for pair in pairs:
        score(0, pair)
    settle(0)
    for b, (_, o_ref, t, _) in enumerate(blocks):
        for pair in pairs:
            if b + 1 < len(blocks):
                score(b + 1, pair)
            mix(b, pair)
        o_ref[t * TILE : (t + 1) * TILE, :] = (mixed[b][:, :HD] / mixed[b][:, HD:]).astype(
            o_ref.dtype
        )
        if b + 1 < len(blocks):
            settle(b + 1)


def attend(allowed, where, arrays, result, chunk_low, far_low, low, high, heads_here):
    queries, q_rec, key, value, kv_rec, rim_a, rim_b, far = arrays
    rows = queries.shape[0]
    slots = allowed.shape[1]
    own = pl.BlockSpec((rows, HD), lambda i, a, w: (0, w[0] * heads_here + low + i))
    flat = pl.BlockSpec((rows, HD), lambda i, a, w: (0, low + i))
    whole = pl.BlockSpec((2, rows, HD), lambda i, a, w: (0, 0, low + i))
    part = pl.BlockSpec((2, rows, HD), lambda i, a, w: (0, 0, low - chunk_low + i))
    tile = pl.BlockSpec((2, TILE, HD), lambda i, a, w: (0, 0, low - far_low + i))
    out = pl.BlockSpec((rows, HD), lambda i, a, w: (0, i))
    shape = jax.ShapeDtypeStruct((rows, (high - low) * HD), queries.dtype)
    inputs = [queries, q_rec, key, value, kv_rec, rim_a, rim_b, *far]
    specs = [own, flat, own, own, part, whole, part] + [tile] * len(far)
    aliases = {}
    kernel = attend_kernel
    if result is not None:
        kernel = functools.partial(skip_operand, attend_kernel, 2 + len(inputs))
        aliases = {2 + len(inputs): 0}
        inputs, specs = inputs + [result], specs + [anywhere]
    return pl.pallas_call(
        kernel,
        out_shape=[jax.ShapeDtypeStruct(queries.shape, queries.dtype), shape],
        grid_spec=pltpu.PrefetchScalarGridSpec(
            num_scalar_prefetch=2,
            grid=(high - low,),
            in_specs=specs,
            out_specs=[own, out],
            scratch_shapes=[
                pltpu.VMEM((slots * TILE, HD), queries.dtype),
                pltpu.VMEM((slots * TILE, 2 * HD), queries.dtype),
                pltpu.VMEM((2, TILE, slots * TILE), jnp.float32),
                pltpu.VMEM((2, TILE, TILE), jnp.float32),
            ],
        ),
        input_output_aliases=aliases,
    )(allowed, where, *inputs)


def skip_operand(kernel, index, *refs):
    kernel(*refs[:index], *refs[index + 1 :])


def place_kernel(lows, heads_here, where, *refs):
    count = len(lows)
    pieces, out, held, sems = refs[:count], refs[count + 1], refs[count + 2 : -1], refs[-1]
    loads, stores = [], []
    for i, low in enumerate(lows):
        cols = pl.ds(pl.multiple_of(((1 - where[0]) * heads_here + low) * HD, HD), held[i].shape[1])
        loads.append(pltpu.make_async_copy(pieces[i], held[i], sems.at[0, i]))
        stores.append(pltpu.make_async_copy(held[i], out.at[:, cols], sems.at[1, i]))
    for load in loads:
        load.start()
    for load, store in zip(loads, stores):
        load.wait()
        store.start()
    for store in stores:
        store.wait()


def place(where, pieces, lows, result, heads_here):
    return pl.pallas_call(
        functools.partial(place_kernel, lows, heads_here),
        out_shape=jax.ShapeDtypeStruct(result.shape, result.dtype),
        grid_spec=pltpu.PrefetchScalarGridSpec(
            num_scalar_prefetch=1,
            grid=(),
            in_specs=[pl.BlockSpec(memory_space=pltpu.HBM)] * (len(pieces) + 1),
            out_specs=anywhere,
            scratch_shapes=[pltpu.VMEM(piece.shape, piece.dtype) for piece in pieces]
            + [pltpu.SemaphoreType.DMA((2, len(pieces)))],
        ),
        input_output_aliases={1 + len(pieces): 0},
    )(where, *pieces, result)


def on_device(queries, key_rows, value_rows, key_tiles, tile_count):
    tok_rows, row_width = queries.shape
    side = lax.axis_index("head")
    slab = lax.axis_index("blk")
    slabs = lax.axis_size("blk")
    group_width = row_width // 2
    heads_here = group_width // HD
    half = tok_rows // TILE
    slab_tiles = 2 * half

    shifts = [(0, slabs // 2)]
    for level in range(2, FAR + 1):
        shifts += [(1, slabs // 2**level), (-1, slabs // 2**level)]
    live = jnp.arange(key_tiles.shape[1], dtype=jnp.int32)[None, :] < tile_count[:, None]
    listed_slab = key_tiles // slab_tiles
    within = key_tiles % slab_tiles
    turned = (within + half * side) % slab_tiles
    mine = jnp.where(live & (listed_slab == slab), turned, 0)
    chosen = jnp.max(mine.reshape(slabs, -1), axis=1)
    readers = [
        (slab + shifts[0][1]) % slabs if direction == 0 else jnp.clip(slab + direction * far, 0, slabs - 1)
        for direction, far in shifts
    ]
    sent_slots = chosen[jnp.stack(readers)]
    where = side.astype(jnp.int32)[None]
    meta = jnp.concatenate([where, sent_slots])

    offset = listed_slab - slab
    slots = jnp.where(offset == 0, turned, -1)
    slots = jnp.where(offset == -1, 2 * half + half * (1 - side) + within - half, slots)
    slots = jnp.where(offset == 1, 2 * half + half * side + within, slots)
    for i, (direction, far) in enumerate(shifts):
        hit = (jnp.abs(offset) == far) if direction == 0 else (offset == -direction * far)
        slots = jnp.where(hit, 4 * half + i, slots)
    slots = jnp.where(live, slots, -1)
    slots = lax.dynamic_slice_in_dim(slots, slab * slab_tiles, slab_tiles, 0)
    slots = jnp.where(side == 0, slots, jnp.roll(slots, half, axis=0))
    slot_total = 4 * half + len(shifts)
    allowed = jnp.any(
        slots[:, :, None] == jnp.arange(slot_total, dtype=jnp.int32)[None, None, :], axis=1
    ).astype(jnp.int32)

    swap = [(0, 1), (1, 0)]
    chunks = chunk_bounds(heads_here)

    def outward(direction):
        return [
            (g * slabs + s, g * slabs + s + step)
            for g, step in ((0, -direction), (1, direction))
            for s in range(slabs)
            if 0 <= s + step < slabs
        ]

    kv_rec = []
    rim_a = None
    for c, (low, high) in enumerate(chunks):
        width = (high - low) * HD
        packed = jnp.stack(
            [columns_of(array, 1 - side, low * HD, width) for array in (key_rows, value_rows)]
        )
        kv_rec.append(lax.ppermute(packed, "head", swap))
        if c == 0:
            rim_a = lax.ppermute(
                jnp.stack(
                    [columns_of(array, side, 0, group_width) for array in (key_rows, value_rows)]
                ),
                ("head", "blk"),
                outward(1),
            )
    q_rec = lax.ppermute(columns_of(queries, 1 - side, 0, group_width), "head", swap)

    rim_b = []
    for c in range(len(chunks)):
        rim_b.append(lax.ppermute(kv_rec[c], ("head", "blk"), outward(-1)))
    far = []
    for members in far_groups:
        low = chunks[members[0]][0]
        tiles = select_distant(
            meta, key_rows, value_rows, [kv_rec[c] for c in members], low * HD, half
        )
        arrived = []
        for (direction, distance), tile in zip(shifts, tiles):
            if direction == 0:
                pairs = [(s, (s + distance) % slabs) for s in range(slabs)]
            else:
                step = direction * distance
                pairs = [(s, s + step) for s in range(slabs) if 0 <= s + step < slabs]
            arrived.append(lax.ppermute(tile, "blk", pairs))
        far += [(low, arrived)] * len(members)
    result, returned = None, []
    for c, a, b in head_runs(heads_here):
        far_low, arrived = far[c]
        arrays = (queries, q_rec, key_rows, value_rows, kv_rec[c], rim_a, rim_b[c], arrived)
        result, sent = attend(
            allowed, where, arrays, result, chunks[c][0], far_low, a, b, heads_here
        )
        returned.append((a, lax.ppermute(sent, "head", swap)))
    result = place(
        where, [p for _, p in returned[:-1]], [a for a, _ in returned[:-1]], result, heads_here
    )
    result = place(where, [returned[-1][1]], [returned[-1][0]], result, heads_here)
    return result


far_groups = ((0,), (1,), (2,))


def chunk_bounds(heads):
    cuts = [0, heads * 3 // 10, heads * 7 // 10, heads]
    return list(zip(cuts[:-1], cuts[1:]))


def head_runs(heads):
    return [(c, low, high) for c, (low, high) in enumerate(chunk_bounds(heads))]


def solution(mesh):
    placed = (
        P(("blk", "head"), None),
        P(("blk", "head"), None),
        P(("blk", "head"), None),
        P(),
        P(),
    )

    return jax.shard_map(
        on_device, mesh=mesh, in_specs=placed, out_specs=P(("blk", "head"), None), check_vma=False
    )
```

```python
import functools
import math

import jax
import jax.numpy as jnp
from jax import lax
from jax.experimental import pallas as pl
from jax.experimental.pallas import tpu as pltpu
from jax.sharding import PartitionSpec as P


HD = 128
TILE = 128
FAR = 3


masked_value = -1e30
exp2_scale = math.log2(math.e) / math.sqrt(HD)
across = (((1,), (1,)), ((), ()))
anywhere = pl.BlockSpec(memory_space=pl.ANY)


def columns_of(array, side, low, width):
    half = array.shape[1] // 2
    first = lax.slice_in_dim(array, low, low + width, axis=1)
    second = lax.slice_in_dim(array, half + low, half + low + width, axis=1)
    return jnp.where(side == 0, first, second)


def pack_kernel(low, flip, where, key, value, out, sems):
    side = 1 - where[0] if flip else where[0]
    first = pl.multiple_of(side * (key.shape[1] // 2) + low, HD)
    copies = [
        pltpu.make_async_copy(source.at[:, pl.ds(first, out.shape[2])], out.at[i], sems.at[i])
        for i, source in enumerate((key, value))
    ]
    for copy in copies:
        copy.start()
    for copy in copies:
        copy.wait()


def pack(where, key, value, low, width, flip):
    return pl.pallas_call(
        functools.partial(pack_kernel, low, flip),
        out_shape=pltpu.VMEM((2, key.shape[0], width), key.dtype),
        grid_spec=pltpu.PrefetchScalarGridSpec(
            num_scalar_prefetch=1,
            grid=(),
            in_specs=[anywhere] * 2,
            out_specs=pl.BlockSpec(memory_space=pltpu.VMEM),
            scratch_shapes=[pltpu.SemaphoreType.DMA((2,))],
        ),
    )(where, key, value)


def distant_kernel(half, jobs, lows, chosen, where, here, key, value, *rest):
    received, outs, sems = rest[: len(lows)], rest[len(lows) : -1], rest[-1]
    slabs = chosen.shape[0]
    side_col = where[0] * (key.shape[1] // 2)
    waits = []
    for i, ((step, members), out) in enumerate(zip(jobs, outs)):
        reader = here[0] + step
        reader = jnp.where(reader < 0, reader + slabs, reader)
        slot = chosen[jnp.where(reader >= slabs, reader - slabs, reader)]
        own = slot < half
        rows = pl.ds(pl.multiple_of(jnp.where(own, slot, slot - half) * TILE, TILE), TILE)
        first = 0
        for p in members:
            part = received[p]
            width = part.shape[2]
            cols = pl.ds(pl.multiple_of(side_col + lows[p], HD), width)
            for j, source in enumerate((key, value)):
                target, sem = out.at[j, :, first : first + width], sems.at[i, j, p]
                mine = pltpu.make_async_copy(source.at[rows, cols], target, sem)
                theirs = pltpu.make_async_copy(part.at[j, rows, :], target, sem)
                pl.when(own)(mine.start)
                pl.when(jnp.logical_not(own))(theirs.start)
                waits.append(theirs)
            first += width
    for copy in waits:
        copy.wait()


def select_distant(chosen, where, here, key, value, received, lows, jobs, half):
    shapes = [
        pltpu.VMEM((2, TILE, sum(received[p].shape[2] for p in members)), key.dtype)
        for _, members in jobs
    ]
    return pl.pallas_call(
        functools.partial(distant_kernel, half, jobs, lows),
        out_shape=shapes,
        grid_spec=pltpu.PrefetchScalarGridSpec(
            num_scalar_prefetch=3,
            grid=(),
            in_specs=[anywhere] * (2 + len(received)),
            out_specs=[pl.BlockSpec(memory_space=pltpu.VMEM)] * len(jobs),
            scratch_shapes=[pltpu.SemaphoreType.DMA((len(jobs), 2, len(received)))],
        ),
    )(chosen, where, here, key, value, *received)


def attend_kernel(allowed, where, q_own, q_rec, k_own, v_own, kv_rec, rim_a, rim_b, *rest):
    far, (o_own, o_send, keys, values, scores, tops) = rest[:-6], rest[-6:]
    rows = q_own.shape[0]
    tiles = rows // TILE
    slots = keys.shape[0] // TILE

    @pl.when(pl.program_id(0) == 0)
    def fill_ones():
        values[:, HD:] = jnp.ones((slots * TILE, HD), values.dtype)

    first = 0
    sources = [(k_own[...], v_own[...])]
    sources += [(ref[0], ref[1]) for ref in (kv_rec, rim_a, rim_b, *far)]
    for key_part, value_part in sources:
        last = first + key_part.shape[0]
        keys[first:last, :] = key_part
        values[first:last, :HD] = value_part
        first = last

    pairs = [(j, min(j + 2, slots)) for j in range(0, slots, 2)]
    blocks = [(q_own, o_own, t, where[0] * tiles + t) for t in range(tiles)]
    blocks += [(q_rec, o_send, t, (1 - where[0]) * tiles + t) for t in range(tiles)]
    largest, mixed = {}, {}

    def score(b, pair):
        q_ref, _, t, row = blocks[b]
        low, high = pair
        cells = lax.dot_general(
            q_ref[t * TILE : (t + 1) * TILE, :],
            keys[low * TILE : high * TILE, :],
            across,
            preferred_element_type=jnp.float32,
        )
        for j in range(low, high):
            cell = cells[:, (j - low) * TILE : (j - low + 1) * TILE]
            cell = jnp.where(allowed[row, j] > 0, cell, masked_value)
            scores[b % 2, :, j * TILE : (j + 1) * TILE] = cell
            largest[b] = cell if b not in largest else jnp.maximum(largest[b], cell)

    def settle(b):
        top = jnp.max(largest[b], axis=-1, keepdims=True)
        tops[b % 2] = jnp.broadcast_to(top, (TILE, TILE))

    def mix(b, pair):
        low, high = pair
        rounded = [
            jnp.exp2(
                (scores[b % 2, :, j * TILE : (j + 1) * TILE] - tops[b % 2]) * exp2_scale
            ).astype(values.dtype)
            for j in range(low, high)
        ]
        part = jnp.dot(
            jnp.concatenate(rounded, 1),
            values[low * TILE : high * TILE, :],
            preferred_element_type=jnp.float32,
        )
        mixed[b] = part if b not in mixed else mixed[b] + part

    for pair in pairs:
        score(0, pair)
    settle(0)
    for b, (_, o_ref, t, _) in enumerate(blocks):
        for pair in pairs:
            if b + 1 < len(blocks):
                score(b + 1, pair)
            mix(b, pair)
        o_ref[t * TILE : (t + 1) * TILE, :] = (mixed[b][:, :HD] / mixed[b][:, HD:]).astype(
            o_ref.dtype
        )
        if b + 1 < len(blocks):
            settle(b + 1)


def attend(allowed, where, arrays, result, chunk_low, far_lows, low, high, heads_here):
    queries, q_rec, key, value, kv_rec, rim_a, rim_b, far = arrays
    rows = queries.shape[0]
    slots = allowed.shape[1]
    own = pl.BlockSpec((rows, HD), lambda i, a, w: (0, w[0] * heads_here + low + i))
    flat = pl.BlockSpec((rows, HD), lambda i, a, w: (0, low + i))
    whole = pl.BlockSpec((2, rows, HD), lambda i, a, w: (0, 0, low + i))
    part = pl.BlockSpec((2, rows, HD), lambda i, a, w: (0, 0, low - chunk_low + i))
    tiles = [
        pl.BlockSpec((2, TILE, HD), lambda i, a, w, start=low - far_low: (0, 0, start + i))
        for far_low in far_lows
    ]
    out = pl.BlockSpec((rows, HD), lambda i, a, w: (0, i))
    shape = jax.ShapeDtypeStruct((rows, (high - low) * HD), queries.dtype)
    inputs = [queries, q_rec, key, value, kv_rec, rim_a, rim_b, *far]
    specs = [own, flat, own, own, part, whole, part] + tiles
    aliases = {}
    kernel = attend_kernel
    if result is not None:
        kernel = functools.partial(skip_operand, attend_kernel, 2 + len(inputs))
        aliases = {2 + len(inputs): 0}
        inputs, specs = inputs + [result], specs + [anywhere]
    return pl.pallas_call(
        kernel,
        out_shape=[jax.ShapeDtypeStruct(queries.shape, queries.dtype), shape],
        grid_spec=pltpu.PrefetchScalarGridSpec(
            num_scalar_prefetch=2,
            grid=(high - low,),
            in_specs=specs,
            out_specs=[own, out],
            scratch_shapes=[
                pltpu.VMEM((slots * TILE, HD), queries.dtype),
                pltpu.VMEM((slots * TILE, 2 * HD), queries.dtype),
                pltpu.VMEM((2, TILE, slots * TILE), jnp.float32),
                pltpu.VMEM((2, TILE, TILE), jnp.float32),
            ],
        ),
        input_output_aliases=aliases,
    )(allowed, where, *inputs)


def skip_operand(kernel, index, *refs):
    kernel(*refs[:index], *refs[index + 1 :])


def place_kernel(lows, heads_here, where, *refs):
    count = len(lows)
    pieces, out, sems = refs[:count], refs[count + 1], refs[-1]
    stores = []
    for i, low in enumerate(lows):
        cols = pl.ds(
            pl.multiple_of(((1 - where[0]) * heads_here + low) * HD, HD), pieces[i].shape[1]
        )
        stores.append(pltpu.make_async_copy(pieces[i], out.at[:, cols], sems.at[i]))
    for store in stores:
        store.start()
    for store in stores:
        store.wait()


def place(where, pieces, lows, result, heads_here):
    pieces = [pltpu.with_memory_space_constraint(piece, pltpu.VMEM) for piece in pieces]
    return pl.pallas_call(
        functools.partial(place_kernel, lows, heads_here),
        out_shape=jax.ShapeDtypeStruct(result.shape, result.dtype),
        grid_spec=pltpu.PrefetchScalarGridSpec(
            num_scalar_prefetch=1,
            grid=(),
            in_specs=[pl.BlockSpec(memory_space=pltpu.VMEM)] * len(pieces) + [anywhere],
            out_specs=anywhere,
            scratch_shapes=[pltpu.SemaphoreType.DMA((len(pieces),))],
        ),
        input_output_aliases={1 + len(pieces): 0},
    )(where, *pieces, result)


def on_device(queries, key_rows, value_rows, key_tiles, tile_count):
    tok_rows, row_width = queries.shape
    side = lax.axis_index("head")
    slab = lax.axis_index("blk")
    slabs = lax.axis_size("blk")
    group_width = row_width // 2
    heads_here = group_width // HD
    half = tok_rows // TILE
    slab_tiles = 2 * half

    shifts = [(0, slabs // 2)]
    for level in range(2, FAR + 1):
        shifts += [(1, slabs // 2**level), (-1, slabs // 2**level)]
    live = jnp.arange(key_tiles.shape[1], dtype=jnp.int32)[None, :] < tile_count[:, None]
    turned = (key_tiles % slab_tiles + half * side) % slab_tiles
    mine = jnp.where(live & (key_tiles // slab_tiles == slab), turned, 0)
    chosen = jnp.max(mine.reshape(slabs, -1), axis=1)
    where = side.astype(jnp.int32)[None]
    here = slab.astype(jnp.int32)[None]

    listed = lax.dynamic_slice_in_dim(key_tiles, slab * slab_tiles, slab_tiles, 0)
    counts = lax.dynamic_slice_in_dim(tile_count, slab * slab_tiles, slab_tiles, 0)
    offset = listed // slab_tiles - slab
    within = listed % slab_tiles
    slots = (within + half * side) % slab_tiles
    slots = jnp.where(offset == -1, 2 * half + half * (1 - side) + within - half, slots)
    slots = jnp.where(offset == 1, 2 * half + half * side + within, slots)
    for i, (direction, far) in enumerate(shifts):
        hit = (jnp.abs(offset) == far) if direction == 0 else (offset == -direction * far)
        slots = jnp.where(hit, 4 * half + i, slots)
    alive = jnp.arange(listed.shape[1], dtype=jnp.int32)[None, :] < counts[:, None]
    slots = jnp.where(alive, slots, -1)
    slot_ids = jnp.arange(4 * half + len(shifts), dtype=jnp.int32)
    allowed = jnp.max((slots[:, :, None] == slot_ids[None, None, :]).astype(jnp.int32), axis=1)

    swap = [(0, 1), (1, 0)]
    chunks = chunk_bounds(heads_here)

    def outward(direction):
        return [
            (g * slabs + s, g * slabs + s + step)
            for g, step in ((0, -direction), (1, direction))
            for s in range(slabs)
            if 0 <= s + step < slabs
        ]

    kv_rec = []
    rim_a = None
    for c, (low, high) in enumerate(chunks):
        width = (high - low) * HD
        if c == 0:
            packed = pack(where, key_rows, value_rows, low * HD, width, True)
        else:
            packed = jnp.stack(
                [columns_of(array, 1 - side, low * HD, width) for array in (key_rows, value_rows)]
            )
        kv_rec.append(lax.ppermute(packed, "head", swap))
        if c == 0:
            rim_a = lax.ppermute(
                pack(where, key_rows, value_rows, 0, group_width, False),
                ("head", "blk"),
                outward(1),
            )
    q_rec = lax.ppermute(columns_of(queries, 1 - side, 0, group_width), "head", swap)

    rim_b = []
    for c in range(len(chunks)):
        rim_b.append(lax.ppermute(kv_rec[c], ("head", "blk"), outward(-1)))
    lows = [low * HD for low, _ in chunks]
    far = [[None] * len(shifts) for _ in chunks]
    for jobs in far_jobs:
        used = sorted({m for _, members in jobs for m in members})
        tiles = select_distant(
            chosen,
            where,
            here,
            key_rows,
            value_rows,
            [kv_rec[m] for m in used],
            [lows[m] for m in used],
            [
                ((shifts[i][0] or 1) * shifts[i][1], tuple(used.index(m) for m in members))
                for i, members in jobs
            ],
            half,
        )
        for (i, members), tile in zip(jobs, tiles):
            direction, distance = shifts[i]
            if direction == 0:
                pairs = [(s, (s + distance) % slabs) for s in range(slabs)]
            else:
                step = direction * distance
                pairs = [(s, s + step) for s in range(slabs) if 0 <= s + step < slabs]
            arrived = lax.ppermute(tile, "blk", pairs)
            for m in members:
                far[m][i] = (chunks[members[0]][0], arrived)
    result, returned = None, []
    for c, a, b in head_runs(heads_here):
        far_lows, arrived = zip(*far[c])
        arrays = (queries, q_rec, key_rows, value_rows, kv_rec[c], rim_a, rim_b[c], arrived)
        result, sent = attend(
            allowed, where, arrays, result, chunks[c][0], far_lows, a, b, heads_here
        )
        returned.append((a, lax.ppermute(sent, "head", swap)))
    result = place(
        where, [p for _, p in returned[:-1]], [a for a, _ in returned[:-1]], result, heads_here
    )
    result = place(where, [returned[-1][1]], [returned[-1][0]], result, heads_here)
    return result


far_jobs = tuple(tuple((i, (c,)) for i in range(2 * FAR - 1)) for c in range(3))


def chunk_bounds(heads):
    cuts = [0, heads * 3 // 10, heads * 7 // 10, heads]
    return list(zip(cuts[:-1], cuts[1:]))


def head_runs(heads):
    return [(c, low, high) for c, (low, high) in enumerate(chunk_bounds(heads))]


def solution(mesh):
    placed = (
        P(("blk", "head"), None),
        P(("blk", "head"), None),
        P(("blk", "head"), None),
        P(),
        P(),
    )

    return jax.shard_map(
        on_device, mesh=mesh, in_specs=placed, out_specs=P(("blk", "head"), None), check_vma=False
    )
```

```python
import functools
import math

import jax
import jax.numpy as jnp
from jax import lax
from jax.experimental import pallas as pl
from jax.experimental.pallas import tpu as pltpu
from jax.sharding import PartitionSpec as P


HD = 128
TILE = 128
FAR = 3


masked_value = -1e30
exp2_scale = math.log2(math.e) / math.sqrt(HD)
across = (((1,), (1,)), ((), ()))
anywhere = pl.BlockSpec(memory_space=pl.ANY)


def columns_of(array, side, low, width):
    half = array.shape[1] // 2
    first = lax.slice_in_dim(array, low, low + width, axis=1)
    second = lax.slice_in_dim(array, half + low, half + low + width, axis=1)
    return jnp.where(side == 0, first, second)


def pack_kernel(low, flip, where, key, value, out, sems):
    side = 1 - where[0] if flip else where[0]
    first = pl.multiple_of(side * (key.shape[1] // 2) + low, HD)
    copies = [
        pltpu.make_async_copy(source.at[:, pl.ds(first, out.shape[2])], out.at[i], sems.at[i])
        for i, source in enumerate((key, value))
    ]
    for copy in copies:
        copy.start()
    for copy in copies:
        copy.wait()


def pack(where, key, value, low, width, flip):
    return pl.pallas_call(
        functools.partial(pack_kernel, low, flip),
        out_shape=pltpu.VMEM((2, key.shape[0], width), key.dtype),
        grid_spec=pltpu.PrefetchScalarGridSpec(
            num_scalar_prefetch=1,
            grid=(),
            in_specs=[anywhere] * 2,
            out_specs=pl.BlockSpec(memory_space=pltpu.VMEM),
            scratch_shapes=[pltpu.SemaphoreType.DMA((2,))],
        ),
    )(where, key, value)


def across_from(slab, distance, near):
    forth = 1 - 2 * lax.rem(lax.div(slab, distance), 2)
    return slab + distance * forth if near else slab - distance * forth


def exchange(slabs, distance, near):
    pairs = []
    for s in range(slabs):
        forth = 1 - 2 * ((s // distance) % 2)
        other = s + distance * forth if near else s - distance * forth
        pairs.append((s, other if 0 <= other < slabs else s ^ 1))
    return pairs


def distant_kernel(half, jobs, lows, chosen, where, here, key, value, *rest):
    received, outs, sems = rest[: len(lows)], rest[len(lows) : -1], rest[-1]
    slabs = chosen.shape[0]
    side_col = where[0] * (key.shape[1] // 2)
    waits = []
    for i, ((step, members), out) in enumerate(zip(jobs, outs)):
        reader = across_from(here[0], *step)
        slot = chosen[jnp.clip(reader, 0, slabs - 1)]
        own = slot < half
        rows = pl.ds(pl.multiple_of(jnp.where(own, slot, slot - half) * TILE, TILE), TILE)
        first = 0
        for p in members:
            part = received[p]
            width = part.shape[2]
            cols = pl.ds(pl.multiple_of(side_col + lows[p], HD), width)
            target = out.at[:, :, first : first + width]
            mine = [
                pltpu.make_async_copy(source.at[rows, cols], target.at[j], sems.at[i, j, p])
                for j, source in enumerate((key, value))
            ]
            theirs = [
                pltpu.make_async_copy(part.at[j, rows, :], target.at[j], sems.at[i, j, p])
                for j in range(2)
            ]
            waits += theirs

            @pl.when(own)
            def from_own(copies=mine):
                for copy in copies:
                    copy.start()

            @pl.when(jnp.logical_not(own))
            def from_received(copies=theirs):
                for copy in copies:
                    copy.start()

            first += width
    for copy in waits:
        copy.wait()


def select_distant(chosen, where, here, key, value, received, lows, jobs, half):
    shapes = [
        pltpu.VMEM((2, TILE, sum(received[p].shape[2] for p in members)), key.dtype)
        for _, members in jobs
    ]
    return pl.pallas_call(
        functools.partial(distant_kernel, half, jobs, lows),
        out_shape=shapes,
        grid_spec=pltpu.PrefetchScalarGridSpec(
            num_scalar_prefetch=3,
            grid=(),
            in_specs=[anywhere] * (2 + len(received)),
            out_specs=[pl.BlockSpec(memory_space=pltpu.VMEM)] * len(jobs),
            scratch_shapes=[pltpu.SemaphoreType.DMA((len(jobs), 2, len(received)))],
        ),
    )(chosen, where, here, key, value, *received)


def attend_kernel(where, allowed, q_own, q_rec, k_own, v_own, kv_rec, rim_a, rim_b, *rest):
    far, (o_own, o_send, keys, values, scores, tops) = rest[:-6], rest[-6:]
    rows = q_own.shape[0]
    tiles = rows // TILE
    slots = keys.shape[0] // TILE

    @pl.when(pl.program_id(0) == 0)
    def fill_ones():
        values[:, HD:] = jnp.ones((slots * TILE, HD), values.dtype)

    first = 0
    sources = [(k_own[...], v_own[...])]
    sources += [(ref[0], ref[1]) for ref in (kv_rec, rim_a, rim_b, *far)]
    for key_part, value_part in sources:
        last = first + key_part.shape[0]
        keys[first:last, :] = key_part
        values[first:last, :HD] = value_part
        first = last

    pairs = [(j, min(j + 2, slots)) for j in range(0, slots, 2)]
    blocks = [(q_own, o_own, t, where[0] * tiles + t) for t in range(tiles)]
    blocks += [(q_rec, o_send, t, (1 - where[0]) * tiles + t) for t in range(tiles)]
    largest, mixed = {}, {}

    def score(b, pair):
        q_ref, _, t, row = blocks[b]
        low, high = pair
        cells = lax.dot_general(
            q_ref[t * TILE : (t + 1) * TILE, :],
            keys[low * TILE : high * TILE, :],
            across,
            preferred_element_type=jnp.float32,
        )
        for j in range(low, high):
            cell = cells[:, (j - low) * TILE : (j - low + 1) * TILE]
            cell = jnp.where(allowed[row, j] > 0, cell, masked_value)
            scores[b % 2, :, j * TILE : (j + 1) * TILE] = cell
            largest[b] = cell if b not in largest else jnp.maximum(largest[b], cell)

    def settle(b):
        top = jnp.max(largest[b], axis=-1, keepdims=True)
        tops[b % 2] = jnp.broadcast_to(top, (TILE, TILE))

    def mix(b, pair):
        low, high = pair
        rounded = [
            jnp.exp2(
                (scores[b % 2, :, j * TILE : (j + 1) * TILE] - tops[b % 2]) * exp2_scale
            ).astype(values.dtype)
            for j in range(low, high)
        ]
        part = jnp.dot(
            jnp.concatenate(rounded, 1),
            values[low * TILE : high * TILE, :],
            preferred_element_type=jnp.float32,
        )
        mixed[b] = part if b not in mixed else mixed[b] + part

    for pair in pairs:
        score(0, pair)
    settle(0)
    for b, (_, o_ref, t, _) in enumerate(blocks):
        for pair in pairs:
            if b + 1 < len(blocks):
                score(b + 1, pair)
            mix(b, pair)
        o_ref[t * TILE : (t + 1) * TILE, :] = (mixed[b][:, :HD] / mixed[b][:, HD:]).astype(
            o_ref.dtype
        )
        if b + 1 < len(blocks):
            settle(b + 1)


def attend(allowed, where, arrays, result, chunk_low, far_lows, low, high, heads_here):
    queries, q_rec, key, value, kv_rec, rim_a, rim_b, far = arrays
    rows = queries.shape[0]
    slots = allowed.shape[1]
    own = pl.BlockSpec((rows, HD), lambda i, w: (0, w[0] * heads_here + low + i))
    flat = pl.BlockSpec((rows, HD), lambda i, w: (0, low + i))
    whole = pl.BlockSpec((2, rows, HD), lambda i, w: (0, 0, low + i))
    part = pl.BlockSpec((2, rows, HD), lambda i, w: (0, 0, low - chunk_low + i))
    tiles = [
        pl.BlockSpec((2, TILE, HD), lambda i, w, start=low - far_low: (0, 0, start + i))
        for far_low in far_lows
    ]
    out = pl.BlockSpec((rows, HD), lambda i, w: (0, i))
    shape = jax.ShapeDtypeStruct((rows, (high - low) * HD), queries.dtype)
    inputs = [allowed, queries, q_rec, key, value, kv_rec, rim_a, rim_b, *far]
    specs = [pl.BlockSpec(memory_space=pltpu.SMEM)]
    specs += [own, flat, own, own, part, whole, part] + tiles
    aliases = {}
    kernel = attend_kernel
    if result is not None:
        kernel = functools.partial(skip_operand, attend_kernel, 1 + len(inputs))
        aliases = {1 + len(inputs): 0}
        inputs, specs = inputs + [result], specs + [anywhere]
    return pl.pallas_call(
        kernel,
        out_shape=[jax.ShapeDtypeStruct(queries.shape, queries.dtype), shape],
        grid_spec=pltpu.PrefetchScalarGridSpec(
            num_scalar_prefetch=1,
            grid=(high - low,),
            in_specs=specs,
            out_specs=[own, out],
            scratch_shapes=[
                pltpu.VMEM((slots * TILE, HD), queries.dtype),
                pltpu.VMEM((slots * TILE, 2 * HD), queries.dtype),
                pltpu.VMEM((2, TILE, slots * TILE), jnp.float32),
                pltpu.VMEM((2, TILE, TILE), jnp.float32),
            ],
        ),
        input_output_aliases=aliases,
    )(where, *inputs)


def skip_operand(kernel, index, *refs):
    kernel(*refs[:index], *refs[index + 1 :])


def place_kernel(lows, heads_here, where, *refs):
    count = len(lows)
    pieces, out, sems = refs[:count], refs[count + 1], refs[-1]
    stores = []
    for i, low in enumerate(lows):
        cols = pl.ds(
            pl.multiple_of(((1 - where[0]) * heads_here + low) * HD, HD), pieces[i].shape[1]
        )
        stores.append(pltpu.make_async_copy(pieces[i], out.at[:, cols], sems.at[i]))
    for store in stores:
        store.start()
    for store in stores:
        store.wait()


def place(where, pieces, lows, result, heads_here):
    pieces = [pltpu.with_memory_space_constraint(piece, pltpu.VMEM) for piece in pieces]
    return pl.pallas_call(
        functools.partial(place_kernel, lows, heads_here),
        out_shape=jax.ShapeDtypeStruct(result.shape, result.dtype),
        grid_spec=pltpu.PrefetchScalarGridSpec(
            num_scalar_prefetch=1,
            grid=(),
            in_specs=[pl.BlockSpec(memory_space=pltpu.VMEM)] * len(pieces) + [anywhere],
            out_specs=anywhere,
            scratch_shapes=[pltpu.SemaphoreType.DMA((len(pieces),))],
        ),
        input_output_aliases={1 + len(pieces): 0},
    )(where, *pieces, result)


def on_device(queries, key_rows, value_rows, key_tiles, tile_count):
    tok_rows, row_width = queries.shape
    side = lax.axis_index("head")
    slab = lax.axis_index("blk")
    slabs = lax.axis_size("blk")
    group_width = row_width // 2
    heads_here = group_width // HD
    half = tok_rows // TILE
    slab_tiles = 2 * half

    shifts = [(slabs // 2, True)]
    for level in range(2, FAR + 1):
        shifts += [(slabs // 2**level, True), (slabs // 2**level, False)]
    live = jnp.arange(key_tiles.shape[1], dtype=jnp.int32)[None, :] < tile_count[:, None]
    turned = (key_tiles % slab_tiles + half * side) % slab_tiles
    mine = jnp.where(live & (key_tiles // slab_tiles == slab), turned, 0)
    chosen = jnp.max(mine.reshape(slabs, -1), axis=1)
    where = side.astype(jnp.int32)[None]
    here = slab.astype(jnp.int32)[None]

    listed = lax.dynamic_slice_in_dim(key_tiles, slab * slab_tiles, slab_tiles, 0)
    counts = lax.dynamic_slice_in_dim(tile_count, slab * slab_tiles, slab_tiles, 0)
    offset = listed // slab_tiles - slab
    within = listed % slab_tiles
    slots = (within + half * side) % slab_tiles
    slots = jnp.where(offset == -1, 2 * half + half * (1 - side) + within - half, slots)
    slots = jnp.where(offset == 1, 2 * half + half * side + within, slots)
    for i, shift in enumerate(shifts):
        slots = jnp.where(listed // slab_tiles == across_from(slab, *shift), 4 * half + i, slots)
    alive = jnp.arange(listed.shape[1], dtype=jnp.int32)[None, :] < counts[:, None]
    slots = jnp.where(alive, slots, -1)
    slot_ids = jnp.arange(4 * half + len(shifts), dtype=jnp.int32)
    allowed = jnp.max((slots[:, :, None] == slot_ids[None, None, :]).astype(jnp.int32), axis=1)

    swap = [(0, 1), (1, 0)]
    chunks = chunk_bounds(heads_here)

    def outward(direction):
        return [
            (g * slabs + s, g * slabs + (s + step) % slabs)
            for g, step in ((0, -direction), (1, direction))
            for s in range(slabs)
        ]

    kv_rec = []
    rim_a = None
    for c, (low, high) in enumerate(chunks):
        width = (high - low) * HD
        if c == 0:
            packed = pack(where, key_rows, value_rows, low * HD, width, True)
        else:
            packed = jnp.stack(
                [columns_of(array, 1 - side, low * HD, width) for array in (key_rows, value_rows)]
            )
        kv_rec.append(lax.ppermute(packed, "head", swap))
        if c == 0:
            rim_a = lax.ppermute(
                pack(where, key_rows, value_rows, 0, group_width, False),
                ("head", "blk"),
                outward(1),
            )
    q_rec = lax.ppermute(columns_of(queries, 1 - side, 0, group_width), "head", swap)

    rim_b = []
    for c in range(len(chunks)):
        rim_b.append(lax.ppermute(kv_rec[c], ("head", "blk"), outward(-1)))
    lows = [low * HD for low, _ in chunks]
    far = [[None] * len(shifts) for _ in chunks]
    for jobs in far_jobs:
        used = sorted({m for _, members in jobs for m in members})
        tiles = select_distant(
            chosen,
            where,
            here,
            key_rows,
            value_rows,
            [kv_rec[m] for m in used],
            [lows[m] for m in used],
            [
                (shifts[i], tuple(used.index(m) for m in members))
                for i, members in jobs
            ],
            half,
        )
        for (i, members), tile in zip(jobs, tiles):
            arrived = lax.ppermute(tile, "blk", exchange(slabs, *shifts[i]))
            for m in members:
                far[m][i] = (chunks[members[0]][0], arrived)
    result, returned = None, []
    for c, a, b in head_runs(heads_here):
        far_lows, arrived = zip(*far[c])
        arrays = (queries, q_rec, key_rows, value_rows, kv_rec[c], rim_a, rim_b[c], arrived)
        result, sent = attend(
            allowed, where, arrays, result, chunks[c][0], far_lows, a, b, heads_here
        )
        returned.append((a, lax.ppermute(sent, "head", swap)))
    result = place(
        where, [p for _, p in returned[:-1]], [a for a, _ in returned[:-1]], result, heads_here
    )
    result = place(where, [returned[-1][1]], [returned[-1][0]], result, heads_here)
    return result


far_jobs = tuple(tuple((i, (c,)) for i in range(2 * FAR - 1)) for c in range(3))


def chunk_bounds(heads):
    cuts = [0, heads * 3 // 10, heads * 7 // 10, heads]
    return list(zip(cuts[:-1], cuts[1:]))


def head_runs(heads):
    first, second, (low, high) = chunk_bounds(heads)
    return [(0, *first), (1, *second), (2, low, high - 1), (2, high - 1, high)]


def solution(mesh):
    placed = (
        P(("blk", "head"), None),
        P(("blk", "head"), None),
        P(("blk", "head"), None),
        P(),
        P(),
    )

    return jax.shard_map(
        on_device, mesh=mesh, in_specs=placed, out_specs=P(("blk", "head"), None), check_vma=False
    )
```

```python
import functools
import math

import jax
import jax.numpy as jnp
from jax import lax
from jax.experimental import pallas as pl
from jax.experimental.pallas import tpu as pltpu
from jax.sharding import PartitionSpec as P


HD = 128
TILE = 128
FAR = 3


masked_value = -1e30
exp2_scale = math.log2(math.e) / math.sqrt(HD)
across = (((1,), (1,)), ((), ()))
anywhere = pl.BlockSpec(memory_space=pl.ANY)


def columns_of(array, side, low, width):
    half = array.shape[1] // 2
    first = lax.slice_in_dim(array, low, low + width, axis=1)
    second = lax.slice_in_dim(array, half + low, half + low + width, axis=1)
    return jnp.where(side == 0, first, second)


def pack_kernel(low, flip, where, key, value, out, sems):
    side = 1 - where[0] if flip else where[0]
    first = pl.multiple_of(side * (key.shape[1] // 2) + low, HD)
    copies = [
        pltpu.make_async_copy(source.at[:, pl.ds(first, out.shape[2])], out.at[i], sems.at[i])
        for i, source in enumerate((key, value))
    ]
    for copy in copies:
        copy.start()
    for copy in copies:
        copy.wait()


def pack(where, key, value, low, width, flip):
    return pl.pallas_call(
        functools.partial(pack_kernel, low, flip),
        out_shape=pltpu.VMEM((2, key.shape[0], width), key.dtype),
        grid_spec=pltpu.PrefetchScalarGridSpec(
            num_scalar_prefetch=1,
            grid=(),
            in_specs=[anywhere] * 2,
            out_specs=pl.BlockSpec(memory_space=pltpu.VMEM),
            scratch_shapes=[pltpu.SemaphoreType.DMA((2,))],
        ),
    )(where, key, value)


def across_from(slab, distance, near):
    forth = 1 - 2 * lax.rem(lax.div(slab, distance), 2)
    return slab + distance * forth if near else slab - distance * forth


def exchange(slabs, distance, near):
    pairs = []
    for s in range(slabs):
        forth = 1 - 2 * ((s // distance) % 2)
        other = s + distance * forth if near else s - distance * forth
        pairs.append((s, other if 0 <= other < slabs else s ^ 1))
    return pairs


def distant_kernel(half, jobs, lows, chosen, where, here, key, value, *rest):
    received, outs, sems = rest[: len(lows)], rest[len(lows) : -1], rest[-1]
    slabs = chosen.shape[0]
    side_col = where[0] * (key.shape[1] // 2)
    waits = []
    for i, ((step, members), out) in enumerate(zip(jobs, outs)):
        reader = across_from(here[0], *step)
        slot = chosen[jnp.clip(reader, 0, slabs - 1)]
        own = slot < half
        rows = pl.ds(pl.multiple_of(jnp.where(own, slot, slot - half) * TILE, TILE), TILE)
        first = 0
        for p in members:
            part = received[p]
            width = part.shape[2]
            cols = pl.ds(pl.multiple_of(side_col + lows[p], HD), width)
            target = out.at[:, :, first : first + width]
            mine = [
                pltpu.make_async_copy(source.at[rows, cols], target.at[j], sems.at[i, j, p])
                for j, source in enumerate((key, value))
            ]
            theirs = [
                pltpu.make_async_copy(part.at[j, rows, :], target.at[j], sems.at[i, j, p])
                for j in range(2)
            ]
            waits += theirs

            @pl.when(own)
            def from_own(copies=mine):
                for copy in copies:
                    copy.start()

            @pl.when(jnp.logical_not(own))
            def from_received(copies=theirs):
                for copy in copies:
                    copy.start()

            first += width
    for copy in waits:
        copy.wait()


def select_distant(chosen, where, here, key, value, received, lows, jobs, half):
    shapes = [
        pltpu.VMEM((2, TILE, sum(received[p].shape[2] for p in members)), key.dtype)
        for _, members in jobs
    ]
    return pl.pallas_call(
        functools.partial(distant_kernel, half, jobs, lows),
        out_shape=shapes,
        grid_spec=pltpu.PrefetchScalarGridSpec(
            num_scalar_prefetch=3,
            grid=(),
            in_specs=[anywhere] * (2 + len(received)),
            out_specs=[pl.BlockSpec(memory_space=pltpu.VMEM)] * len(jobs),
            scratch_shapes=[pltpu.SemaphoreType.DMA((len(jobs), 2, len(received)))],
        ),
    )(chosen, where, here, key, value, *received)


def attend_kernel(where, allowed, q_own, q_rec, k_own, v_own, kv_rec, rim_a, rim_b, *rest):
    far, (o_own, o_send, keys, values, scores, tops) = rest[:-6], rest[-6:]
    rows = q_own.shape[0]
    tiles = rows // TILE
    slots = keys.shape[0] // TILE

    @pl.when(pl.program_id(0) == 0)
    def fill_ones():
        values[:, HD:] = jnp.ones((slots * TILE, HD), values.dtype)

    first = 0
    sources = [(k_own[...], v_own[...])]
    sources += [(ref[0], ref[1]) for ref in (kv_rec, rim_a, rim_b, *far)]
    for key_part, value_part in sources:
        last = first + key_part.shape[0]
        keys[first:last, :] = key_part
        values[first:last, :HD] = value_part
        first = last

    pairs = [(j, min(j + 2, slots)) for j in range(0, slots, 2)]
    blocks = [(q_own, o_own, t, where[0] * tiles + t) for t in range(tiles)]
    blocks += [(q_rec, o_send, t, (1 - where[0]) * tiles + t) for t in range(tiles)]
    largest, mixed = {}, {}

    def score(b, pair):
        q_ref, _, t, row = blocks[b]
        low, high = pair
        cells = lax.dot_general(
            q_ref[t * TILE : (t + 1) * TILE, :],
            keys[low * TILE : high * TILE, :],
            across,
            preferred_element_type=jnp.float32,
        )
        for j in range(low, high):
            cell = cells[:, (j - low) * TILE : (j - low + 1) * TILE]
            cell = jnp.where(allowed[row, j] > 0, cell, masked_value)
            scores[b % 2, :, j * TILE : (j + 1) * TILE] = cell
            largest[b] = cell if b not in largest else jnp.maximum(largest[b], cell)

    def settle(b):
        top = jnp.max(largest[b], axis=-1, keepdims=True)
        tops[b % 2] = jnp.broadcast_to(top, (TILE, TILE))

    def mix(b, pair):
        low, high = pair
        rounded = [
            jnp.exp2(
                (scores[b % 2, :, j * TILE : (j + 1) * TILE] - tops[b % 2]) * exp2_scale
            ).astype(values.dtype)
            for j in range(low, high)
        ]
        part = jnp.dot(
            jnp.concatenate(rounded, 1),
            values[low * TILE : high * TILE, :],
            preferred_element_type=jnp.float32,
        )
        mixed[b] = part if b not in mixed else mixed[b] + part

    for pair in pairs:
        score(0, pair)
    settle(0)
    for b, (_, o_ref, t, _) in enumerate(blocks):
        for pair in pairs:
            if b + 1 < len(blocks):
                score(b + 1, pair)
            mix(b, pair)
        o_ref[t * TILE : (t + 1) * TILE, :] = (mixed[b][:, :HD] / mixed[b][:, HD:]).astype(
            o_ref.dtype
        )
        if b + 1 < len(blocks):
            settle(b + 1)


def attend(allowed, where, arrays, result, chunk_low, q_low, far_lows, low, high, heads_here):
    queries, q_rec, key, value, kv_rec, rim_a, rim_b, far = arrays
    rows = queries.shape[0]
    slots = allowed.shape[1]
    own = pl.BlockSpec((rows, HD), lambda i, w: (0, w[0] * heads_here + low + i))
    asked = pl.BlockSpec((rows, HD), lambda i, w: (0, low - q_low + i))
    whole = pl.BlockSpec((2, rows, HD), lambda i, w: (0, 0, low + i))
    part = pl.BlockSpec((2, rows, HD), lambda i, w: (0, 0, low - chunk_low + i))
    tiles = [
        pl.BlockSpec((2, TILE, HD), lambda i, w, start=low - far_low: (0, 0, start + i))
        for far_low in far_lows
    ]
    out = pl.BlockSpec((rows, HD), lambda i, w: (0, i))
    shape = jax.ShapeDtypeStruct((rows, (high - low) * HD), queries.dtype)
    inputs = [allowed, queries, q_rec, key, value, kv_rec, rim_a, rim_b, *far]
    specs = [pl.BlockSpec(memory_space=pltpu.SMEM)]
    specs += [own, asked, own, own, part, whole, part] + tiles
    aliases = {}
    kernel = attend_kernel
    if result is not None:
        kernel = functools.partial(skip_operand, attend_kernel, 1 + len(inputs))
        aliases = {1 + len(inputs): 0}
        inputs, specs = inputs + [result], specs + [anywhere]
    return pl.pallas_call(
        kernel,
        out_shape=[jax.ShapeDtypeStruct(queries.shape, queries.dtype), shape],
        grid_spec=pltpu.PrefetchScalarGridSpec(
            num_scalar_prefetch=1,
            grid=(high - low,),
            in_specs=specs,
            out_specs=[own, out],
            scratch_shapes=[
                pltpu.VMEM((slots * TILE, HD), queries.dtype),
                pltpu.VMEM((slots * TILE, 2 * HD), queries.dtype),
                pltpu.VMEM((2, TILE, slots * TILE), jnp.float32),
                pltpu.VMEM((2, TILE, TILE), jnp.float32),
            ],
        ),
        input_output_aliases=aliases,
    )(where, *inputs)


def skip_operand(kernel, index, *refs):
    kernel(*refs[:index], *refs[index + 1 :])


def place_kernel(lows, heads_here, where, *refs):
    count = len(lows)
    pieces, out, sems = refs[:count], refs[count + 1], refs[-1]
    stores = []
    for i, low in enumerate(lows):
        cols = pl.ds(
            pl.multiple_of(((1 - where[0]) * heads_here + low) * HD, HD), pieces[i].shape[1]
        )
        stores.append(pltpu.make_async_copy(pieces[i], out.at[:, cols], sems.at[i]))
    for store in stores:
        store.start()
    for store in stores:
        store.wait()


def place(where, pieces, lows, result, heads_here):
    pieces = [pltpu.with_memory_space_constraint(piece, pltpu.VMEM) for piece in pieces]
    return pl.pallas_call(
        functools.partial(place_kernel, lows, heads_here),
        out_shape=jax.ShapeDtypeStruct(result.shape, result.dtype),
        grid_spec=pltpu.PrefetchScalarGridSpec(
            num_scalar_prefetch=1,
            grid=(),
            in_specs=[pl.BlockSpec(memory_space=pltpu.VMEM)] * len(pieces) + [anywhere],
            out_specs=anywhere,
            scratch_shapes=[pltpu.SemaphoreType.DMA((len(pieces),))],
        ),
        input_output_aliases={1 + len(pieces): 0},
    )(where, *pieces, result)


def on_device(queries, key_rows, value_rows, key_tiles, tile_count):
    tok_rows, row_width = queries.shape
    side = lax.axis_index("head")
    slab = lax.axis_index("blk")
    slabs = lax.axis_size("blk")
    group_width = row_width // 2
    heads_here = group_width // HD
    half = tok_rows // TILE
    slab_tiles = 2 * half

    shifts = [(slabs // 2, True)]
    for level in range(2, FAR + 1):
        shifts += [(slabs // 2**level, True), (slabs // 2**level, False)]
    live = jnp.arange(key_tiles.shape[1], dtype=jnp.int32)[None, :] < tile_count[:, None]
    turned = (key_tiles % slab_tiles + half * side) % slab_tiles
    mine = jnp.where(live & (key_tiles // slab_tiles == slab), turned, 0)
    chosen = jnp.max(mine.reshape(slabs, -1), axis=1)
    where = side.astype(jnp.int32)[None]
    here = slab.astype(jnp.int32)[None]

    listed = lax.dynamic_slice_in_dim(key_tiles, slab * slab_tiles, slab_tiles, 0)
    counts = lax.dynamic_slice_in_dim(tile_count, slab * slab_tiles, slab_tiles, 0)
    offset = listed // slab_tiles - slab
    within = listed % slab_tiles
    slots = (within + half * side) % slab_tiles
    slots = jnp.where(offset == -1, 2 * half + half * (1 - side) + within - half, slots)
    slots = jnp.where(offset == 1, 2 * half + half * side + within, slots)
    for i, shift in enumerate(shifts):
        slots = jnp.where(listed // slab_tiles == across_from(slab, *shift), 4 * half + i, slots)
    alive = jnp.arange(listed.shape[1], dtype=jnp.int32)[None, :] < counts[:, None]
    slots = jnp.where(alive, slots, -1)
    slot_ids = jnp.arange(4 * half + len(shifts), dtype=jnp.int32)
    allowed = jnp.max((slots[:, :, None] == slot_ids[None, None, :]).astype(jnp.int32), axis=1)

    swap = [(0, 1), (1, 0)]
    chunks = chunk_bounds(heads_here)

    def outward(direction):
        return [
            (g * slabs + s, g * slabs + (s + step) % slabs)
            for g, step in ((0, -direction), (1, direction))
            for s in range(slabs)
        ]

    kv_rec = []
    rim_a = None
    for c, (low, high) in enumerate(chunks):
        width = (high - low) * HD
        if c == 0:
            packed = pack(where, key_rows, value_rows, low * HD, width, True)
        else:
            packed = jnp.stack(
                [columns_of(array, 1 - side, low * HD, width) for array in (key_rows, value_rows)]
            )
        kv_rec.append(lax.ppermute(packed, "head", swap))
        if c == 0:
            rim_a = lax.ppermute(
                pack(where, key_rows, value_rows, 0, group_width, False),
                ("head", "blk"),
                outward(1),
            )
    q_rec = []
    for low, high in ((0, chunks[0][1]), (chunks[0][1], heads_here)):
        asked = columns_of(queries, 1 - side, low * HD, (high - low) * HD)
        q_rec.append((low, lax.ppermute(asked, "head", swap)))

    rim_b = []
    for c in range(len(chunks)):
        rim_b.append(lax.ppermute(kv_rec[c], ("head", "blk"), outward(-1)))
    lows = [low * HD for low, _ in chunks]
    far = [[None] * len(shifts) for _ in chunks]
    for jobs in far_jobs:
        used = sorted({m for _, members in jobs for m in members})
        tiles = select_distant(
            chosen,
            where,
            here,
            key_rows,
            value_rows,
            [kv_rec[m] for m in used],
            [lows[m] for m in used],
            [
                (shifts[i], tuple(used.index(m) for m in members))
                for i, members in jobs
            ],
            half,
        )
        for (i, members), tile in zip(jobs, tiles):
            arrived = lax.ppermute(tile, "blk", exchange(slabs, *shifts[i]))
            for m in members:
                far[m][i] = (chunks[members[0]][0], arrived)
    result, returned = None, []
    for c, a, b in head_runs(heads_here):
        far_lows, arrived = zip(*far[c])
        q_low, q_part = q_rec[min(c, 1)]
        arrays = (queries, q_part, key_rows, value_rows, kv_rec[c], rim_a, rim_b[c], arrived)
        result, sent = attend(
            allowed, where, arrays, result, chunks[c][0], q_low, far_lows, a, b, heads_here
        )
        returned.append((a, lax.ppermute(sent, "head", swap)))
    result = place(
        where, [p for _, p in returned[:-1]], [a for a, _ in returned[:-1]], result, heads_here
    )
    result = place(where, [returned[-1][1]], [returned[-1][0]], result, heads_here)
    return result


far_jobs = tuple(tuple((i, (c,)) for i in range(2 * FAR - 1)) for c in range(4))


def chunk_bounds(heads):
    cuts = [0, heads * 2 // 10, heads * 5 // 10, heads * 8 // 10, heads]
    return list(zip(cuts[:-1], cuts[1:]))


def head_runs(heads):
    return [(c, low, high) for c, (low, high) in enumerate(chunk_bounds(heads))]


def solution(mesh):
    placed = (
        P(("blk", "head"), None),
        P(("blk", "head"), None),
        P(("blk", "head"), None),
        P(),
        P(),
    )

    return jax.shard_map(
        on_device, mesh=mesh, in_specs=placed, out_specs=P(("blk", "head"), None), check_vma=False
    )
```
